256 devices in a mesh: gx: 8 (over x, z_lo), gy: 4 (over z_hi), ta: 8 (over y, core).
Axes of the slice: x: 4, y: 4, z: 8 (z_hi: 4, z_lo: 2; z = z_hi * 2 + z_lo), core: 2. Of those that a mesh axis runs over, the one named last changes fastest.
Arguments:
- traces: bfloat16 [1048576, 1024], P(('gx', 'gy'), 'ta'), may hold values from -6 to 6
- interp: bfloat16 [2, 16], replicated, may hold values from -1.5 to 1.5
- translations: bfloat16 [4, 2048, 1024], P(None, ('gx', 'gy')), may hold values from -0.125 to 0.125
- leaf_slot: int32 [65536], P(('gx', 'gy', 'ta')), may hold values from 0 to 255, as said below
- pairing: int32 [4, 65536], P(None, ('gx', 'gy', 'ta')), may hold values from 0 to 255, as said below
Outputs:
- coefficients: bfloat16 [65536, 1024], P(('gx', 'gy', 'ta'))
The draws below stay inside these ranges and needn't reach their ends.
Inputs may be any that keep to these rules, and one draw needn't show every extreme that they name: `leaf_slot`: each aligned block of 256 entries (the leaves of one device) is a permutation of 0 to 255. `pairing`: for every level, each aligned block of 256 entries along the leaves is a permutation of 0 to 255.
All inputs are finite; a program needn't handle non-finite values.
Results may differ from the reference program's by a relative error of at most 0.0082.
Values may be sent and summed in bfloat16 or wider, within the bound.
No kernel may reach another device: no remote copies, remote signals or barrier semaphores. Data moves between devices by JAX's collectives and lax.ppermute only.
A program may use at most 128 MiB of HBM per device.

```python
import math
import jax
import jax.numpy as jnp
from jax import lax

NT = 1024
NF = 256
CHEB = 2
BOXT = 16
LEVELS = 4
BOX_DEV = 256
W = 1024
NBOX = 65536
NTRACE = 1048576
N_GX = 8
N_GY = 4
N_TA = 8


def block_perms(key, blocks, width):
    keys = jax.random.split(key, blocks)
    return jax.vmap(lambda subkey: jax.random.permutation(subkey, width))(keys).astype(jnp.int32)


def draw_leaf_slot(key, part):
    return block_perms(jax.random.fold_in(key, 11), NBOX // BOX_DEV, BOX_DEV).reshape(NBOX)


def draw_pairing(key, part):
    return block_perms(jax.random.fold_in(key, 23), LEVELS * (NBOX // BOX_DEV), BOX_DEV).reshape(LEVELS, NBOX)


def levels(key, shape, cuts, least, largest):
    loudness = 1.0
    for dim, parts in cuts:
        draws = jax.random.uniform(jax.random.fold_in(jax.random.fold_in(key, 6), dim), (parts,), jnp.float32, least / len(cuts), largest / len(cuts))
        loudness = loudness * jnp.repeat(jnp.exp(draws), shape[dim] // parts).reshape((-1,) + (1,) * (len(shape) - 1 - dim))
    return loudness


def scatter_about(key, extent, scale, limit, pieces=(), kind=jnp.bfloat16):
    level = levels(key, extent, pieces, -0.22, 0.18) if pieces else 1.0
    values = jax.random.normal(key, extent, jnp.float32) * scale * level
    return jnp.minimum(jnp.maximum(values, -limit), limit).astype(kind)


def setup_inputs(seed: int = 0) -> dict:
    splits = jax.random.split(jax.random.key(seed), 6)
    return {
        "traces": scatter_about(splits[0], (NTRACE, NT), 1.0, 6.0, ((0, 32), (1, 8))),
        "interp": scatter_about(splits[1], (CHEB, BOXT), BOXT ** -0.5, 1.5),
        "translations": scatter_about(splits[2], (LEVELS, 2 * W, W), (2 * W) ** -0.5, 0.125, ((1, 32),)),
        "leaf_slot": draw_leaf_slot(jax.random.fold_in(splits[5], 71), 0),
        "pairing": draw_pairing(jax.random.fold_in(splits[5], 71), 0),
    }


def spectrum_table(length, count):
    sample_pos = lax.broadcasted_iota(jnp.float32, (length, count), 0)
    frequency = lax.broadcasted_iota(jnp.float32, (length, count), 1) + 1.0
    angles = 2.0 * math.pi / length * jnp.mod(sample_pos * frequency, float(length))
    factor = math.sqrt(2.0 / length)
    return jnp.concatenate([jnp.cos(angles) * factor, -jnp.sin(angles) * factor], axis=1).astype(jnp.bfloat16)

def reference(traces, interp, translations, leaf_slot, pairing):
    devices = N_GX * N_GY * N_TA
    groups = N_GX * N_GY
    per_peer = BOX_DEV // groups
    fourier = spectrum_table(NT, NF)
    weights = interp.astype(jnp.float32)

    def one_device(device_block):
        sampled = jnp.einsum('cb,kbt->kct', weights, device_block.astype(jnp.float32), precision=lax.Precision.HIGHEST)
        sampled = sampled.astype(jnp.bfloat16).reshape(BOX_DEV * CHEB, NT)
        spectra = jnp.dot(sampled, fourier, preferred_element_type=jnp.float32)
        return spectra.reshape(BOX_DEV, CHEB * 2 * NF).astype(jnp.bfloat16)
    cheb_points = lax.map(one_device, traces.reshape(devices, BOX_DEV, BOXT, NT))
    cheb_points = cheb_points.reshape(NBOX, CHEB * 2 * NF)
    leaves = jnp.arange(NBOX, dtype=jnp.int32)
    owners = leaves // BOX_DEV
    group_index = owners // N_TA
    ta_index = owners % N_TA
    source_group = leaf_slot // per_peer
    offset = leaf_slot % per_peer
    source_rows = ((source_group * N_TA + ta_index) * BOX_DEV + group_index * per_peer + offset).astype(jnp.int32)
    states = cheb_points[source_rows]
    log_devices = devices.bit_length() - 1
    for layer_index in range(LEVELS):
        flip_bit = layer_index * log_devices // LEVELS
        partner = ((owners ^ 1 << flip_bit) * BOX_DEV + pairing[layer_index]).astype(jnp.int32)
        joined = jnp.concatenate([states, states[partner]], axis=1).astype(jnp.float32)
        product_sum = jnp.dot(joined, translations[layer_index].astype(jnp.float32), precision=lax.Precision.HIGHEST)
        states = product_sum.astype(jnp.bfloat16)
    return states
```

```python
import functools
import math

import jax
import jax.numpy as jnp
from jax import lax
from jax.experimental import pallas as pl
from jax.experimental.pallas import tpu as pltpu
from jax.sharding import Mesh
from jax.sharding import PartitionSpec as P

NF = 256
CHEB = 2
BOXT = 16
AXES = ("x", "zl", "zh", "y", "c")
GROUP = ("x", "zl", "zh")
TA = ("y", "c")
BF16 = jnp.bfloat16
F32 = jnp.float32
VMEM_LIMIT = 12 << 20
SHORT = 1 << 28
LONG = 1 << 37


def spectrum_table(length, count):
    step = 32
    frequency = lax.broadcasted_iota(jnp.int32, (step, count), 1) + 1
    digit = lax.broadcasted_iota(jnp.int32, (step, count), 0)
    low = (2.0 * math.pi / length) * ((digit * frequency) % length).astype(F32)
    high = (2.0 * math.pi / length) * ((digit * step * frequency) % length).astype(F32)
    factor = math.sqrt(2.0 / length)
    cos_low, sin_low = jnp.cos(low)[None], jnp.sin(low)[None]
    cos_high, sin_high = (jnp.cos(high) * factor)[:, None], (jnp.sin(high) * factor)[:, None]
    real = (cos_high * cos_low - sin_high * sin_low).reshape(length, count)
    imag = (sin_high * cos_low + cos_high * sin_low).reshape(length, count)
    return jnp.concatenate([real, -imag], axis=1).astype(BF16)


def flip(value, mask):
    size = lax.axis_size(AXES)
    return lax.ppermute(value, AXES, [(i, i ^ mask) for i in range(size)])


def shifted(value, axis, k):
    size = lax.axis_size(axis)
    return lax.ppermute(value, axis, [(i, (i + k) % size) for i in range(size)])


def pieces_from(value, axis):
    size = lax.axis_size(axis)
    away = {k: shifted(value, axis, k) for k in (2, 1, 3)}
    return [value if k == 0 else away[k] for k in range(size)]


def doubled(value, mask, bit):
    there = flip(value, mask)
    low = jnp.where(bit == 0, value, there)
    high = jnp.where(bit == 0, there, value)
    return jnp.concatenate([low, high], axis=0)


def select_rows(index, values):
    rows = values.shape[0]
    picks = lax.broadcasted_iota(jnp.int32, (index.shape[0], rows), 1) == index
    hot = jnp.where(picks, 1.0, 0.0).astype(BF16)
    return jnp.dot(hot, values, preferred_element_type=F32).astype(BF16)


def plan_copies(layout, place, mine, other, weights):
    x, y, c = place[0], place[1], place[2]
    copies = []
    for half, source in enumerate((mine, other)):
        column = jnp.where(c == half, 0, 512)
        for k in range(4):
            rows = pl.ds(pl.multiple_of(lax.rem(x + (4 - k), 4) * 512, 512), 512)
            if layout == "x":
                cols = pl.ds(pl.multiple_of(column, 512), 512)
                copies.append((source.at[k], weights.at[rows, cols]))
            else:
                for j in range(4):
                    cols = pl.ds(pl.multiple_of(column + lax.rem(y + (4 - j), 4) * 128, 128), 128)
                    copies.append((source.at[j, k], weights.at[rows, cols]))
    return copies


def near_body(layout, place, own, mine, other, weights, partial, sems):
    started = []
    for n, (source, target) in enumerate(plan_copies(layout, place, mine, other, weights)):
        copy = pltpu.make_async_copy(source, target, sems.at[n])
        copy.start()
        started.append(copy)
    for copy in started:
        copy.wait()
    for n in range(4):
        cols = slice(n * 256, (n + 1) * 256)
        partial[:, cols] = jnp.dot(own[...], weights[:1024, cols], preferred_element_type=F32)


def far_body(index, far, weights, partial, out):
    aligned = select_rows(index[...], far[...])
    for n in range(4):
        cols = slice(n * 256, (n + 1) * 256)
        total = jnp.dot(aligned, weights[1024:, cols], preferred_element_type=F32)
        out[:, cols] = (total + partial[:, cols]).astype(BF16)


def select_body(index, values, out):
    out[...] = select_rows(index[...], values[...])


def spectrum_body(sampled, table, out):
    out[...] = jnp.dot(sampled[...], table[...], preferred_element_type=F32).astype(BF16)


VMEM = pl.BlockSpec(memory_space=pltpu.VMEM)
HBM = pl.BlockSpec(memory_space=pltpu.HBM)


def on_chip(body, shape, flops, name, *operands):
    return pl.pallas_call(
        body,
        out_shape=jax.ShapeDtypeStruct(shape, BF16),
        in_specs=[VMEM] * len(operands),
        out_specs=VMEM,
        compiler_params=pltpu.CompilerParams(vmem_limit_bytes=VMEM_LIMIT),
        cost_estimate=pl.CostEstimate(flops=flops, bytes_accessed=1 << 20, transcendentals=0),
        name=name,
    )(*operands)


def near_step(level, layout, place, own, mine):
    other = flip(mine, 1)
    mine, other = [pltpu.with_memory_space_constraint(piece, pltpu.HBM) for piece in (mine, other)]
    return pl.pallas_call(
        functools.partial(near_body, layout),
        out_shape=[jax.ShapeDtypeStruct((2048, 1024), BF16), jax.ShapeDtypeStruct(own.shape, F32)],
        in_specs=[pl.BlockSpec(memory_space=pltpu.SMEM), VMEM, HBM, HBM],
        out_specs=[VMEM, VMEM],
        scratch_shapes=[pltpu.SemaphoreType.DMA((8 if layout == "x" else 32,))],
        compiler_params=pltpu.CompilerParams(vmem_limit_bytes=VMEM_LIMIT),
        cost_estimate=pl.CostEstimate(flops=256 * 2048 * 1024, bytes_accessed=6 << 20, transcendentals=0),
        name="near" + str(level),
    )(place, own, mine, other)


def far_step(level, index, far, joined, partial):
    return on_chip(far_body, far.shape, 256 * 2048 * 1024, "far" + str(level), index, far, joined, partial)


def on_device(traces, interp, translations, leaf_slot, pairing):
    x, y, c = lax.axis_index("x"), lax.axis_index("y"), lax.axis_index("c")
    zl, zh = lax.axis_index("zl"), lax.axis_index("zh")
    together = lax.optimization_barrier
    place = jnp.stack([x, y, c]).astype(jnp.int32)

    def column(values):
        return values.reshape(values.shape[0], 1)

    def half(level):
        return lax.dynamic_slice_in_dim(translations[level], c * 512, 512, 1)

    def eighth(level):
        return lax.dynamic_slice_in_dim(translations[level], c * 512 + y * 128, 128, 1)

    rows = doubled(jnp.concatenate([half(0), eighth(1), eighth(3), half(2)], axis=1), 8, zh % 2)
    early, late = rows[:, :768], rows[:, 768:]
    local_boxes = traces.shape[0] // BOXT
    local_cols = traces.shape[1]
    sampled = jnp.einsum(
        "cb,kbt->kct", interp, traces.reshape(local_boxes, BOXT, local_cols), preferred_element_type=F32
    )
    sampled = sampled.astype(BF16).reshape(local_boxes * CHEB, local_cols)
    sampled, early, late = together((sampled, early, late))

    sampled = lax.all_to_all(sampled, TA, split_axis=0, concat_axis=1, tiled=True)
    early = doubled(doubled(early, 16, zh // 2), 32, zl)
    w0, w13 = early[:, :512], early[:, 512:]
    fourier = spectrum_table(sampled.shape[1], NF)
    leaf_index, *pair_index = [column(values) for values in (leaf_slot, *pairing)]
    points = on_chip(
        spectrum_body, (sampled.shape[0], fourier.shape[1]), LONG, "spectrum", sampled, fourier
    ).reshape(sampled.shape[0] // CHEB, CHEB * 2 * NF)
    points, w0, w13, late, leaf_index, pair_index = together((points, w0, w13, late, leaf_index, pair_index))

    states = lax.all_to_all(points, GROUP, split_axis=0, concat_axis=0, tiled=True)
    w13 = pieces_from(w13, "x")
    w1 = jnp.stack([piece[:, :128] for piece in w13])
    w3 = jnp.stack([piece[:, 128:] for piece in w13])
    w1 = jnp.stack(pieces_from(w1, "y"))
    w0 = jnp.stack(pieces_from(w0, "x"))
    late = doubled(late, 16, zh // 2)
    states = on_chip(select_body, states.shape, LONG, "leaves", leaf_index, states)
    states, w0, w1, w3, late = together((states, w0, w1, w3, late))

    far = flip(states, 1)
    w2 = doubled(late, 32, zl)
    joined, partial = near_step(0, "x", place, states, w0)
    far, w2 = together((far, w2))
    states = far_step(0, pair_index[0], far, joined, partial)

    far = flip(states, 4)
    states, w2 = together((states, w2))
    w2 = jnp.stack(pieces_from(w2, "x"))
    joined, partial = near_step(1, "y", place, states, w1)
    far, w2 = together((far, w2))
    states = far_step(1, pair_index[1], far, joined, partial)

    far = flip(states, 16)
    states, w3 = together((states, w3))
    w3 = jnp.stack(pieces_from(w3, "y"))
    joined, partial = near_step(2, "x", place, states, w2)
    far, w3 = together((far, w3))
    states = far_step(2, pair_index[2], far, joined, partial)

    far = flip(states, 64)
    joined, partial = near_step(3, "y", place, states, w3)
    return far_step(3, pair_index[3], far, joined, partial)


def solution(mesh):
    split = Mesh(mesh.devices.reshape(4, 2, 4, 4, 2), AXES)
    placed = (P(GROUP, TA), P(), P(None, GROUP, None), P(AXES), P(None, AXES))
    return jax.shard_map(on_device, mesh=split, in_specs=placed, out_specs=P(AXES, None), check_vma=False)
```

```python
import functools
import math

import jax
import jax.numpy as jnp
from jax import lax
from jax.experimental import pallas as pl
from jax.experimental.pallas import tpu as pltpu
from jax.sharding import Mesh
from jax.sharding import PartitionSpec as P

NF = 256
CHEB = 2
BOXT = 16
AXES = ("x", "zl", "zh", "y", "c")
GROUP = ("x", "zl", "zh")
TA = ("y", "c")
BF16 = jnp.bfloat16
F32 = jnp.float32
VMEM_LIMIT = 12 << 20
SHORT = 1 << 28
LONG = 1 << 37


def spectrum_table(length, count):
    step = 32
    frequency = lax.broadcasted_iota(jnp.int32, (step, count), 1) + 1
    digit = lax.broadcasted_iota(jnp.int32, (step, count), 0)
    low = (2.0 * math.pi / length) * ((digit * frequency) % length).astype(F32)
    high = (2.0 * math.pi / length) * ((digit * step * frequency) % length).astype(F32)
    factor = math.sqrt(2.0 / length)
    cos_low, sin_low = jnp.cos(low)[None], jnp.sin(low)[None]
    cos_high, sin_high = (jnp.cos(high) * factor)[:, None], (jnp.sin(high) * factor)[:, None]
    real = (cos_high * cos_low - sin_high * sin_low).reshape(length, count)
    imag = (sin_high * cos_low + cos_high * sin_low).reshape(length, count)
    return jnp.concatenate([real, -imag], axis=1).astype(BF16)


def flip(value, mask):
    size = lax.axis_size(AXES)
    return lax.ppermute(value, AXES, [(i, i ^ mask) for i in range(size)])


def shifted(value, axis, k):
    size = lax.axis_size(axis)
    return lax.ppermute(value, axis, [(i, (i + k) % size) for i in range(size)])


def pieces_from(value, axis):
    size = lax.axis_size(axis)
    away = {k: shifted(value, axis, k) for k in (2, 1, 3)}
    return [value if k == 0 else away[k] for k in range(size)]


def doubled(value, mask, bit):
    there = flip(value, mask)
    low = jnp.where(bit == 0, value, there)
    high = jnp.where(bit == 0, there, value)
    return jnp.concatenate([low, high], axis=0)


def select_rows(index, values):
    rows = values.shape[0]
    picks = lax.broadcasted_iota(jnp.int32, (index.shape[0], rows), 1) == index
    hot = jnp.where(picks, 1.0, 0.0).astype(BF16)
    return jnp.dot(hot, values, preferred_element_type=F32).astype(BF16)


def plan_copies(level, place, mine, other, weights):
    x, y, c = place[0], place[1], place[2]
    copies = []
    for half, sources in enumerate((mine, other)):
        column = jnp.where(c == half, 0, 512)
        for source in sources:
            if len(source.shape) == 5:
                cols = pl.ds(pl.multiple_of(column, 512), 512)
                for n in range(4):
                    for z in range(8):
                        row = lax.rem(x + (4 - n), 4) * 512 + (z % 2 * 4 + z // 2) * 64
                        rows = pl.ds(pl.multiple_of(row, 64), 64)
                        copies.append((source.at[z, n, level - 2], weights.at[rows, cols]))
        for k in range(4):
            rows = pl.ds(pl.multiple_of(lax.rem(x + (4 - k), 4) * 512, 512), 512)
            for n, source in enumerate(sources):
                if len(source.shape) == 3:
                    width = source.shape[2]
                    cols = pl.ds(pl.multiple_of(column + n * width, 256), width)
                    copies.append((source.at[k], weights.at[rows, cols]))
                elif len(source.shape) == 4:
                    for j in range(4):
                        cols = pl.ds(pl.multiple_of(column + lax.rem(y + (4 - j), 4) * 128, 128), 128)
                        copies.append((source.at[j, k], weights.at[rows, cols]))
    return copies


def near_body(level, count, place, own, *refs):
    mine, other = refs[:count], refs[count : 2 * count]
    weights, partial, sems = refs[2 * count :]
    started = []
    for n, (source, target) in enumerate(plan_copies(level, place, mine, other, weights)):
        copy = pltpu.make_async_copy(source, target, sems.at[n])
        copy.start()
        started.append(copy)
    for copy in started:
        copy.wait()
    for n in range(4):
        cols = slice(n * 256, (n + 1) * 256)
        partial[:, cols] = jnp.dot(own[...], weights[:1024, cols], preferred_element_type=F32)


def far_body(index, far, weights, partial, out):
    aligned = select_rows(index[...], far[...])
    for n in range(4):
        cols = slice(n * 256, (n + 1) * 256)
        total = jnp.dot(aligned, weights[1024:, cols], preferred_element_type=F32)
        out[:, cols] = (total + partial[:, cols]).astype(BF16)


def select_body(index, values, out):
    out[...] = select_rows(index[...], values[...])


def spectrum_body(sampled, table, out):
    out[...] = jnp.dot(sampled[...], table[...], preferred_element_type=F32).astype(BF16)


VMEM = pl.BlockSpec(memory_space=pltpu.VMEM)
HBM = pl.BlockSpec(memory_space=pltpu.HBM)


def on_chip(body, shape, flops, name, *operands):
    return pl.pallas_call(
        body,
        out_shape=jax.ShapeDtypeStruct(shape, BF16),
        in_specs=[VMEM] * len(operands),
        out_specs=VMEM,
        compiler_params=pltpu.CompilerParams(vmem_limit_bytes=VMEM_LIMIT),
        cost_estimate=pl.CostEstimate(flops=flops, bytes_accessed=1 << 20, transcendentals=0),
        name=name,
    )(*operands)


def near_step(level, place, own, mine, other):
    pieces = [pltpu.with_memory_space_constraint(piece, pltpu.HBM) for piece in (*mine, *other)]
    copies = sum({5: 32, 3: 4, 4: 16}[piece.ndim] for piece in pieces)
    return pl.pallas_call(
        functools.partial(near_body, level, len(mine)),
        out_shape=[jax.ShapeDtypeStruct((2048, 1024), BF16), jax.ShapeDtypeStruct(own.shape, F32)],
        in_specs=[pl.BlockSpec(memory_space=pltpu.SMEM), VMEM] + [HBM] * len(pieces),
        out_specs=[VMEM, VMEM],
        scratch_shapes=[pltpu.SemaphoreType.DMA((copies,))],
        compiler_params=pltpu.CompilerParams(vmem_limit_bytes=VMEM_LIMIT),
        cost_estimate=pl.CostEstimate(flops=256 * 2048 * 1024, bytes_accessed=6 << 20, transcendentals=0),
        name="near" + str(level),
    )(place, own, *pieces)


def far_step(level, index, far, joined, partial):
    return on_chip(far_body, far.shape, 256 * 2048 * 1024, "far" + str(level), index, far, joined, partial)


def on_device(traces, interp, translations, leaf_slot, pairing):
    x, y, c = lax.axis_index("x"), lax.axis_index("y"), lax.axis_index("c")
    zl, zh = lax.axis_index("zl"), lax.axis_index("zh")
    together = lax.optimization_barrier
    place = jnp.stack([x, y, c]).astype(jnp.int32)

    def column(values):
        return values.reshape(values.shape[0], 1)

    def half(level):
        return lax.dynamic_slice_in_dim(translations[level], c * 512, 512, 1)

    def eighth(level):
        return lax.dynamic_slice_in_dim(translations[level], c * 512 + y * 128, 128, 1)

    late = jnp.stack(pieces_from(jnp.stack([half(2), half(3)]), "x"))
    rows = doubled(jnp.concatenate([half(0), eighth(1)], axis=1), 8, zh % 2)
    local_boxes = traces.shape[0] // BOXT
    local_cols = traces.shape[1]
    sampled = jnp.einsum(
        "cb,kbt->kct", interp, traces.reshape(local_boxes, BOXT, local_cols), preferred_element_type=F32
    )
    sampled = sampled.astype(BF16).reshape(local_boxes * CHEB, local_cols)
    sampled, rows = together((sampled, rows))

    sampled = lax.all_to_all(sampled, TA, split_axis=0, concat_axis=1, tiled=True)
    rows = doubled(doubled(rows, 16, zh // 2), 32, zl)
    w0, w1 = rows[:, :512], rows[:, 512:]
    fourier = spectrum_table(sampled.shape[1], NF)
    leaf_index, *pair_index = [column(values) for values in (leaf_slot, *pairing)]
    points = on_chip(
        spectrum_body, (sampled.shape[0], fourier.shape[1]), LONG, "spectrum", sampled, fourier
    ).reshape(sampled.shape[0] // CHEB, CHEB * 2 * NF)
    points, w0, w1, late, leaf_index, pair_index = together((points, w0, w1, late, leaf_index, pair_index))

    states = lax.all_to_all(points, GROUP, split_axis=0, concat_axis=0, tiled=True)
    w1 = jnp.stack(pieces_from(w1, "x"))
    w1 = jnp.stack(pieces_from(w1, "y"))
    w0 = jnp.stack(pieces_from(w0, "x"))
    states = on_chip(select_body, states.shape, SHORT, "leaves", leaf_index, states)
    states, w0, w1 = together((states, w0, w1))

    late = lax.all_gather(late, ("zh", "zl"))
    others = {}
    for level, mask in enumerate((1, 4, 16, 64)):
        far = flip(states, mask)
        if level == 2:
            states, late = together((states, late))
            others[2] = others[3] = flip(late, 1)
        elif level < 2:
            states, w1 = together((states, w1))
            others[level] = flip((w0, w1)[level], 1)
        joined, partial = near_step(level, place, states, [(w0, w1, late, late)[level]], [others[level]])
        states = far_step(level, pair_index[level], far, joined, partial)
    return states


def solution(mesh):
    split = Mesh(mesh.devices.reshape(4, 2, 4, 4, 2), AXES)
    placed = (P(GROUP, TA), P(), P(None, GROUP, None), P(AXES), P(None, AXES))
    return jax.shard_map(on_device, mesh=split, in_specs=placed, out_specs=P(AXES, None), check_vma=False)
```

```python
import functools
import math

import jax
import jax.numpy as jnp
from jax import lax
from jax.experimental import pallas as pl
from jax.experimental.pallas import tpu as pltpu
from jax.sharding import Mesh
from jax.sharding import PartitionSpec as P

NF = 256
CHEB = 2
BOXT = 16
AXES = ("x", "zl", "zh", "y", "c")
GROUP = ("x", "zl", "zh")
TA = ("y", "c")
BF16 = jnp.bfloat16
F32 = jnp.float32
VMEM_LIMIT = 12 << 20
SHORT = 1 << 28
LONG = 1 << 37


def spectrum_table(length, count):
    step = 32
    frequency = lax.broadcasted_iota(jnp.int32, (step, count), 1) + 1
    digit = lax.broadcasted_iota(jnp.int32, (step, count), 0)
    low = (2.0 * math.pi / length) * ((digit * frequency) % length).astype(F32)
    high = (2.0 * math.pi / length) * ((digit * step * frequency) % length).astype(F32)
    factor = math.sqrt(2.0 / length)
    cos_low, sin_low = jnp.cos(low)[None], jnp.sin(low)[None]
    cos_high, sin_high = (jnp.cos(high) * factor)[:, None], (jnp.sin(high) * factor)[:, None]
    real = (cos_high * cos_low - sin_high * sin_low).reshape(length, count)
    imag = (sin_high * cos_low + cos_high * sin_low).reshape(length, count)
    return jnp.concatenate([real, -imag], axis=1).astype(BF16)


def flip(value, mask):
    size = lax.axis_size(AXES)
    return lax.ppermute(value, AXES, [(i, i ^ mask) for i in range(size)])


def shifted(value, axis, k):
    size = lax.axis_size(axis)
    return lax.ppermute(value, axis, [(i, (i + k) % size) for i in range(size)])


def pieces_from(value, axis):
    size = lax.axis_size(axis)
    away = {k: shifted(value, axis, k) for k in (2, 1, 3)}
    return [value if k == 0 else away[k] for k in range(size)]


def doubled(value, mask, bit):
    there = flip(value, mask)
    low = jnp.where(bit == 0, value, there)
    high = jnp.where(bit == 0, there, value)
    return jnp.concatenate([low, high], axis=0)


def select_rows(index, values):
    rows = values.shape[0]
    picks = lax.broadcasted_iota(jnp.int32, (index.shape[0], rows), 1) == index
    hot = jnp.where(picks, 1.0, 0.0).astype(BF16)
    return jnp.dot(hot, values, preferred_element_type=F32).astype(BF16)


def plan_copies(level, place, mine, other, weights):
    x, c = place[0], place[1]
    copies = []
    for half, source in enumerate((mine, other)):
        cols = pl.ds(pl.multiple_of(jnp.where(c == half, 0, 512), 512), 512)
        for k in range(4):
            start = lax.rem(x + (4 - k), 4) * 512
            if len(source.shape) == 3:
                rows = pl.ds(pl.multiple_of(start, 512), 512)
                copies.append((source.at[k], weights.at[rows, cols]))
                continue
            for z in range(8):
                rows = pl.ds(pl.multiple_of(start + (z % 2 * 4 + z // 2) * 64, 64), 64)
                block = source.at[z, k] if level == 1 else source.at[z, k, level - 2]
                copies.append((block, weights.at[rows, cols]))
    return copies


def near_body(level, place, own, mine, other, weights, partial, sems):
    started = []
    for n, (source, target) in enumerate(plan_copies(level, place, mine, other, weights)):
        copy = pltpu.make_async_copy(source, target, sems.at[n])
        copy.start()
        started.append(copy)
    for copy in started:
        copy.wait()
    for n in range(4):
        cols = slice(n * 256, (n + 1) * 256)
        partial[:, cols] = jnp.dot(own[...], weights[:1024, cols], preferred_element_type=F32)


def far_body(index, far, weights, partial, out):
    aligned = select_rows(index[...], far[...])
    for n in range(4):
        cols = slice(n * 256, (n + 1) * 256)
        total = jnp.dot(aligned, weights[1024:, cols], preferred_element_type=F32)
        out[:, cols] = (total + partial[:, cols]).astype(BF16)


def copy_body(values, out):
    out[...] = values[...]


def select_body(index, values, out):
    out[...] = select_rows(index[...], values[...])


def spectrum_body(sampled, table, out):
    out[...] = jnp.dot(sampled[...], table[...], preferred_element_type=F32).astype(BF16)


VMEM = pl.BlockSpec(memory_space=pltpu.VMEM)
HBM = pl.BlockSpec(memory_space=pltpu.HBM)


def on_chip(body, shape, flops, name, *operands):
    return pl.pallas_call(
        body,
        out_shape=jax.ShapeDtypeStruct(shape, BF16),
        in_specs=[VMEM] * len(operands),
        out_specs=VMEM,
        compiler_params=pltpu.CompilerParams(vmem_limit_bytes=VMEM_LIMIT),
        cost_estimate=pl.CostEstimate(flops=flops, bytes_accessed=1 << 20, transcendentals=0),
        name=name,
    )(*operands)


def near_step(level, place, own, mine, other):
    mine, other = [pltpu.with_memory_space_constraint(piece, pltpu.HBM) for piece in (mine, other)]
    copies = 8 if mine.ndim == 3 else 64
    return pl.pallas_call(
        functools.partial(near_body, level),
        out_shape=[jax.ShapeDtypeStruct((2048, 1024), BF16), jax.ShapeDtypeStruct(own.shape, F32)],
        in_specs=[pl.BlockSpec(memory_space=pltpu.SMEM), VMEM, HBM, HBM],
        out_specs=[VMEM, VMEM],
        scratch_shapes=[pltpu.SemaphoreType.DMA((copies,))],
        compiler_params=pltpu.CompilerParams(vmem_limit_bytes=VMEM_LIMIT),
        cost_estimate=pl.CostEstimate(flops=256 * 2048 * 1024, bytes_accessed=6 << 20, transcendentals=0),
        name="near" + str(level),
    )(place, own, mine, other)


def far_step(level, index, far, joined, partial):
    return on_chip(far_body, far.shape, 256 * 2048 * 1024, "far" + str(level), index, far, joined, partial)


def on_device(traces, interp, translations, leaf_slot, pairing):
    x, c = lax.axis_index("x"), lax.axis_index("c")
    zl, zh = lax.axis_index("zl"), lax.axis_index("zh")
    together = lax.optimization_barrier
    place = jnp.stack([x, c]).astype(jnp.int32)

    def column(values):
        return values.reshape(values.shape[0], 1)

    half = lax.dynamic_slice_in_dim(translations, c * 512, 512, 2)
    late = pieces_from(half[1:], "x")
    rows = doubled(half[0], 8, zh % 2)
    local_boxes = traces.shape[0] // BOXT
    local_cols = traces.shape[1]
    sampled = jnp.einsum(
        "cb,kbt->kct", interp, traces.reshape(local_boxes, BOXT, local_cols), preferred_element_type=F32
    )
    sampled = sampled.astype(BF16).reshape(local_boxes * CHEB, local_cols)
    sampled, rows, late = together((sampled, rows, late))
    late = jnp.stack(late)

    sampled = lax.all_to_all(sampled, TA, split_axis=0, concat_axis=1, tiled=True)
    w0 = doubled(doubled(rows, 16, zh // 2), 32, zl)
    fourier = spectrum_table(sampled.shape[1], NF)
    leaf_index, *pair_index = [column(values) for values in (leaf_slot, *pairing)]
    points = on_chip(
        spectrum_body, (sampled.shape[0], fourier.shape[1]), LONG, "spectrum", sampled, fourier
    ).reshape(sampled.shape[0] // CHEB, CHEB * 2 * NF)
    points, w0, leaf_index, pair_index = together((points, w0, leaf_index, pair_index))

    states = lax.all_to_all(points, GROUP, split_axis=0, concat_axis=0, tiled=True)
    w1 = lax.all_gather(late[:, 0], ("zh", "zl"))
    w0 = jnp.stack(pieces_from(w0, "x"))
    states = on_chip(select_body, states.shape, SHORT, "leaves", leaf_index, states)
    states, w0, w1 = together((states, w0, w1))

    w23 = lax.all_gather(late[:, 1:], ("zh", "zl"))
    others = {0: flip(w0, 1)}
    for level, mask in enumerate((1, 4, 16, 64)):
        far = flip(states, mask)
        if level == 1:
            states, w1 = together((states, w1))
            others[1] = flip(w1, 1)
        elif level == 2:
            states, w23 = together((states, w23))
            others[2] = others[3] = flip(w23, 1)
        joined, partial = near_step(level, place, states, (w0, w1, w23, w23)[level], others[level])
        if level == 2:
            far = on_chip(copy_body, far.shape, LONG, "arrived2", far)
        states = far_step(level, pair_index[level], far, joined, partial)
    return states


def solution(mesh):
    split = Mesh(mesh.devices.reshape(4, 2, 4, 4, 2), AXES)
    placed = (P(GROUP, TA), P(), P(None, GROUP, None), P(AXES), P(None, AXES))
    return jax.shard_map(on_device, mesh=split, in_specs=placed, out_specs=P(AXES, None), check_vma=False)
```

```python
import functools
import math

import jax
import jax.numpy as jnp
from jax import lax
from jax.experimental import pallas as pl
from jax.experimental.pallas import tpu as pltpu
from jax.sharding import Mesh
from jax.sharding import PartitionSpec as P

NF = 256
CHEB = 2
BOXT = 16
AXES = ("x", "zl", "zh", "y", "c")
GROUP = ("x", "zl", "zh")
TA = ("y", "c")
BF16 = jnp.bfloat16
F32 = jnp.float32
VMEM_LIMIT = 12 << 20
SHORT = 1 << 28
LONG = 1 << 37


def spectrum_table(length, count):
    step = 32
    frequency = lax.broadcasted_iota(jnp.int32, (step, count), 1) + 1
    digit = lax.broadcasted_iota(jnp.int32, (step, count), 0)
    low = (2.0 * math.pi / length) * ((digit * frequency) % length).astype(F32)
    high = (2.0 * math.pi / length) * ((digit * step * frequency) % length).astype(F32)
    factor = math.sqrt(2.0 / length)
    cos_low, sin_low = jnp.cos(low)[None], jnp.sin(low)[None]
    cos_high, sin_high = (jnp.cos(high) * factor)[:, None], (jnp.sin(high) * factor)[:, None]
    real = (cos_high * cos_low - sin_high * sin_low).reshape(length, count)
    imag = (sin_high * cos_low + cos_high * sin_low).reshape(length, count)
    return jnp.concatenate([real, -imag], axis=1).astype(BF16)


def flip(value, mask):
    size = lax.axis_size(AXES)
    return lax.ppermute(value, AXES, [(i, i ^ mask) for i in range(size)])


def shifted(value, axis, k):
    size = lax.axis_size(axis)
    return lax.ppermute(value, axis, [(i, (i + k) % size) for i in range(size)])


def pieces_from(value, axis):
    size = lax.axis_size(axis)
    away = {k: shifted(value, axis, k) for k in (2, 1, 3)}
    return [value if k == 0 else away[k] for k in range(size)]


def doubled(value, mask, bit):
    there = flip(value, mask)
    low = jnp.where(bit == 0, value, there)
    high = jnp.where(bit == 0, there, value)
    return jnp.concatenate([low, high], axis=0)


def select_rows(index, values):
    rows = values.shape[0]
    picks = lax.broadcasted_iota(jnp.int32, (index.shape[0], rows), 1) == index
    hot = jnp.where(picks, 1.0, 0.0).astype(BF16)
    return jnp.dot(hot, values, preferred_element_type=F32).astype(BF16)


def plan_copies(level, place, mine, other, weights):
    x, c = place[0], place[1]
    copies = []
    for half, source in enumerate((mine, other)):
        cols = pl.ds(pl.multiple_of(jnp.where(c == half, 0, 512), 512), 512)
        for k in range(4):
            start = lax.rem(x + (4 - k), 4) * 512
            if len(source.shape) == 3:
                rows = pl.ds(pl.multiple_of(start, 512), 512)
                copies.append((source.at[k], weights.at[rows, cols]))
                continue
            for z in range(8):
                rows = pl.ds(pl.multiple_of(start + (z % 2 * 4 + z // 2) * 64, 64), 64)
                block = source.at[z, k] if level == 1 else source.at[z, k, level - 2]
                copies.append((block, weights.at[rows, cols]))
    return copies


def near_body(level, place, own, mine, other, weights, partial, sems):
    started = []
    for n, (source, target) in enumerate(plan_copies(level, place, mine, other, weights)):
        copy = pltpu.make_async_copy(source, target, sems.at[n])
        copy.start()
        started.append(copy)
    for copy in started:
        copy.wait()
    for n in range(4):
        cols = slice(n * 256, (n + 1) * 256)
        partial[:, cols] = jnp.dot(own[...], weights[:1024, cols], preferred_element_type=F32)


def far_body(index, far, weights, partial, out):
    aligned = select_rows(index[...], far[...])
    for n in range(4):
        cols = slice(n * 256, (n + 1) * 256)
        total = jnp.dot(aligned, weights[1024:, cols], preferred_element_type=F32)
        out[:, cols] = (total + partial[:, cols]).astype(BF16)


def select_body(index, values, out):
    out[...] = select_rows(index[...], values[...])


def spectrum_body(sampled, table, out):
    out[...] = jnp.dot(sampled[...], table[...], preferred_element_type=F32).astype(BF16)


VMEM = pl.BlockSpec(memory_space=pltpu.VMEM)
HBM = pl.BlockSpec(memory_space=pltpu.HBM)


def on_chip(body, shape, flops, name, *operands):
    return pl.pallas_call(
        body,
        out_shape=jax.ShapeDtypeStruct(shape, BF16),
        in_specs=[VMEM] * len(operands),
        out_specs=VMEM,
        compiler_params=pltpu.CompilerParams(vmem_limit_bytes=VMEM_LIMIT),
        cost_estimate=pl.CostEstimate(flops=flops, bytes_accessed=1 << 20, transcendentals=0),
        name=name,
    )(*operands)


def near_step(level, place, own, mine, other):
    mine, other = [pltpu.with_memory_space_constraint(piece, pltpu.HBM) for piece in (mine, other)]
    copies = 8 if mine.ndim == 3 else 64
    return pl.pallas_call(
        functools.partial(near_body, level),
        out_shape=[jax.ShapeDtypeStruct((2048, 1024), BF16), jax.ShapeDtypeStruct(own.shape, F32)],
        in_specs=[pl.BlockSpec(memory_space=pltpu.SMEM), VMEM, HBM, HBM],
        out_specs=[VMEM, VMEM],
        scratch_shapes=[pltpu.SemaphoreType.DMA((copies,))],
        compiler_params=pltpu.CompilerParams(vmem_limit_bytes=VMEM_LIMIT),
        cost_estimate=pl.CostEstimate(flops=256 * 2048 * 1024, bytes_accessed=6 << 20, transcendentals=0),
        name="near" + str(level),
    )(place, own, mine, other)


def far_step(level, index, far, joined, partial):
    return on_chip(far_body, far.shape, 256 * 2048 * 1024, "far" + str(level), index, far, joined, partial)


def on_device(traces, interp, translations, leaf_slot, pairing):
    x, c = lax.axis_index("x"), lax.axis_index("c")
    zl, zh = lax.axis_index("zl"), lax.axis_index("zh")
    together = lax.optimization_barrier
    place = jnp.stack([x, c]).astype(jnp.int32)

    def column(values):
        return values.reshape(values.shape[0], 1)

    half = lax.dynamic_slice_in_dim(translations, c * 512, 512, 2)
    late = pieces_from(half[1:], "x")
    rows = doubled(half[0], 8, zh % 2)
    local_boxes = traces.shape[0] // BOXT
    local_cols = traces.shape[1]
    sampled = jnp.einsum(
        "cb,kbt->kct", interp, traces.reshape(local_boxes, BOXT, local_cols), preferred_element_type=F32
    )
    sampled = sampled.astype(BF16).reshape(local_boxes * CHEB, local_cols)
    sampled, rows, late = together((sampled, rows, late))
    late = jnp.stack(late)

    sampled = lax.all_to_all(sampled, TA, split_axis=0, concat_axis=1, tiled=True)
    w0 = doubled(doubled(rows, 16, zh // 2), 32, zl)
    fourier = spectrum_table(sampled.shape[1], NF)
    leaf_index, *pair_index = [column(values) for values in (leaf_slot, *pairing)]
    points = on_chip(
        spectrum_body, (sampled.shape[0], fourier.shape[1]), LONG, "spectrum", sampled, fourier
    ).reshape(sampled.shape[0] // CHEB, CHEB * 2 * NF)
    points, w0, leaf_index, pair_index = together((points, w0, leaf_index, pair_index))

    states = lax.all_to_all(points, GROUP, split_axis=0, concat_axis=0, tiled=True)
    w1 = lax.all_gather(late[:, 0], ("zh", "zl"))
    w0 = jnp.stack(pieces_from(w0, "x"))
    states = on_chip(select_body, states.shape, SHORT, "leaves", leaf_index, states)
    states, w0, w1 = together((states, w0, w1))

    w23 = lax.all_gather(late[:, 1:], ("zh", "zl"))
    others = {0: flip(w0, 1)}
    for level, mask in enumerate((1, 4, 16, 64)):
        far = flip(states, mask)
        if level == 1:
            states, w1 = together((states, w1))
            others[1] = flip(w1, 1)
        elif level == 2:
            states, w23 = together((states, w23))
            others[2] = others[3] = flip(w23, 1)
        joined, partial = near_step(level, place, states, (w0, w1, w23, w23)[level], others[level])
        states = far_step(level, pair_index[level], far, joined, partial)
    return states


def solution(mesh):
    split = Mesh(mesh.devices.reshape(4, 2, 4, 4, 2), AXES)
    placed = (P(GROUP, TA), P(), P(None, GROUP, None), P(AXES), P(None, AXES))
    return jax.shard_map(on_device, mesh=split, in_specs=placed, out_specs=P(AXES, None), check_vma=False)
```
